32 devices in a mesh: slab: 2 (over x), pair: 8 (over z, y), quad: 2 (over core).
Axes of the slice: x: 2, y: 2, z: 4, core: 2. Of those that a mesh axis runs over, the one named last changes fastest.
Arguments:
- interferograms: float32 [64, 512, 1024], P(('pair', 'quad'), 'slab'), parts along dimension 1, may hold values from -24 to 24
- pair_epochs: int32 [2, 64], replicated, may hold values from 0 to 31, as said below
- days: int32 [32], replicated, may hold values from 0 to 732, as said below
Outputs:
- smoothed: float32 [32, 512, 1024], P(None, ('slab', 'pair'), 'quad'), parts along dimension 1
The draws below stay inside these ranges and needn't reach their ends.
There are 2 independent parts, one for each index of `slab`. The reference program is written for one: setup_inputs(seed, part) draws one part's arguments, and reference() takes and returns one part's arrays. A program takes and returns all parts, laid end to end along the dimension named above; an argument that names none is the same for every part. Nothing has to cross between parts.
Inputs may be any that keep to these rules, and one draw needn't show every extreme that they name: pair_epochs[0, p] < pair_epochs[1, p] for every pair, the difference is at most 8, and every two consecutive epochs e, e + 1 form one of the pairs. days are strictly increasing, days[0] = 0, consecutive days differ by 12, 24 or 36, and the last day is always the maximum.
All inputs are finite; a program needn't handle non-finite values.
Results may differ from the reference program's by a relative error of at most 0.000071.
Values sent between devices are 32-bit elements; how exact they have to be, the bound alone decides.
No kernel may reach another device: no remote copies, remote signals or barrier semaphores. Data moves between devices by JAX's collectives and lax.ppermute only.
A program may use at most 64 MiB of HBM per device.

```python
import jax
import jax.numpy as jnp
from jax import lax

P_SIZE = 64
E = 32
RADIUS = 6
H = 256
W = 1024


def draw_pair_epochs(key, part):
    base = jax.random.fold_in(key, 11)
    key_span, key_start, key_order = jax.random.split(base, 3)
    extra = P_SIZE - (E - 1)
    chain_first = jnp.arange(E - 1).astype(jnp.int32)
    chain_second = chain_first + 1
    spans = jax.random.randint(key_span, (extra,), 2, 9).astype(jnp.int32)
    starts = jax.random.randint(key_start, (extra,), 0, 1 << 20).astype(jnp.int32) % (E - spans)
    first = jnp.concatenate([chain_first, starts])
    second = jnp.concatenate([chain_second, starts + spans])
    order = jax.random.permutation(key_order, P_SIZE)
    return jnp.stack([first[order], second[order]]).astype(jnp.int32)


def draw_days(key, part):
    base = jax.random.fold_in(key, 23)
    shuffled = jax.random.permutation(base, E - 1).astype(jnp.int32)
    gaps = 12 * (1 + shuffled % 3)
    return jnp.concatenate([jnp.zeros((1,), jnp.int32), jnp.cumsum(gaps)]).astype(jnp.int32)


def block_levels(own_key, extent, pieces, smallest, largest):
    gain, own = 1.0, jax.random.fold_in(own_key, 6)
    for axis_at, parts in pieces:
        heights = jnp.exp(jax.random.uniform(jax.random.fold_in(own, axis_at), (parts,), jnp.float32, smallest / len(pieces), largest / len(pieces)))
        gain = gain * jnp.repeat(heights, extent[axis_at] // parts).reshape([-1 if axis == axis_at else 1 for axis in range(len(extent))])
    return gain


def gaussian(rng, dims, scale, bound, cuts=(), kind=jnp.bfloat16):
    loudness = block_levels(rng, dims, cuts, -0.22, 0.18) if cuts else 1.0
    array = jax.random.normal(rng, dims, jnp.float32) * scale * loudness
    return jnp.minimum(jnp.maximum(array, -bound), bound).astype(kind)


def setup_inputs(seed: int = 0, part: int = 0) -> dict:
    streams_of = jax.random.split(jax.random.key(seed), 4)
    part_keys = jax.random.split(jax.random.fold_in(streams_of[3], part), 4)
    interferograms = gaussian(part_keys[0], (P_SIZE, H, W), 3.0, 24.0, ((0, 16),), jnp.float32)
    pair_epochs = draw_pair_epochs(jax.random.fold_in(streams_of[3], 71), part)
    days = draw_days(jax.random.fold_in(streams_of[3], 71), part)
    return {"interferograms": interferograms, "pair_epochs": pair_epochs, "days": days}


def pseudo_inverse(pair_epochs):
    first = pair_epochs[0].astype(jnp.int32)
    second = pair_epochs[1].astype(jnp.int32)
    steps_idx = jnp.arange(E - 1).astype(jnp.int32)
    design = ((first[:, None] <= steps_idx[None, :]) & (steps_idx[None, :] < second[:, None])).astype(jnp.float32)
    normal = jnp.dot(design.T, design, precision=lax.Precision.HIGHEST)
    factor = jnp.linalg.cholesky(normal)
    return jax.scipy.linalg.cho_solve((factor, True), design.T)

def trend_basis(days):
    times = days.astype(jnp.float32)
    scaled = (times - jnp.mean(times)) / 365.25
    phase = 2.0 * jnp.pi * times / 365.25
    basis = jnp.stack([jnp.ones_like(times), scaled, jnp.sin(phase), jnp.cos(phase)], axis=1)
    factor = jnp.linalg.cholesky(jnp.dot(basis.T, basis, precision=lax.Precision.HIGHEST))
    return (basis, factor)

def gauss_taps():
    offsets = (jnp.arange(2 * RADIUS + 1) - RADIUS).astype(jnp.float32)
    weights = jnp.exp(-offsets * offsets / 8.0)
    return weights / jnp.sum(weights)

def reference(interferograms, pair_epochs, days):
    height = interferograms.shape[1]
    width = interferograms.shape[2]
    flat = interferograms.reshape(P_SIZE, height * width)
    pinv = pseudo_inverse(pair_epochs)
    increments = jnp.dot(pinv, flat, precision=lax.Precision.HIGHEST)
    displacement = jnp.concatenate([jnp.zeros((1, height * width), jnp.float32), jnp.cumsum(increments, axis=0)], axis=0)
    basis, factor = trend_basis(days)
    coefficients = jax.scipy.linalg.cho_solve((factor, True), jnp.dot(basis.T, displacement, precision=lax.Precision.HIGHEST))
    detrended = displacement - jnp.dot(basis, coefficients, precision=lax.Precision.HIGHEST)
    detrended = detrended.reshape(E, height, width)
    taps = gauss_taps()
    padded = jnp.pad(detrended, ((0, 0), (0, 0), (RADIUS, RADIUS)))
    across = taps[0] * padded[:, :, 0:width]
    for shift in range(1, 2 * RADIUS + 1):
        across = across + taps[shift] * padded[:, :, shift:shift + width]
    padded = jnp.pad(across, ((0, 0), (RADIUS, RADIUS), (0, 0)))
    smoothed = taps[0] * padded[:, 0:height, :]
    for shift in range(1, 2 * RADIUS + 1):
        smoothed = smoothed + taps[shift] * padded[:, shift:shift + height, :]
    return smoothed
```

```python
import functools

import jax
import jax.numpy as jnp
from jax import lax
from jax.experimental import pallas as pl
from jax.experimental.pallas import tpu as pltpu
from jax.sharding import PartitionSpec as P

E = 32
RADIUS = 6
SUB = 8
LANE = 128
HIGHEST = lax.Precision.HIGHEST


def pseudo_inverse(pair_epochs):
    first = pair_epochs[0]
    second = pair_epochs[1]
    steps_idx = jnp.arange(E - 1)
    design = (
        (first[:, None] <= steps_idx[None, :]) & (steps_idx[None, :] < second[:, None])
    ).astype(jnp.float32)
    normal = jnp.dot(design.T, design, precision=HIGHEST)
    factor = jnp.linalg.cholesky(normal)
    return jax.scipy.linalg.cho_solve((factor, True), design.T)


def trend_basis(days):
    times = days.astype(jnp.float32)
    scaled = (times - jnp.mean(times)) / 365.25
    phase = 2.0 * jnp.pi * times / 365.25
    basis = jnp.stack([jnp.ones_like(times), scaled, jnp.sin(phase), jnp.cos(phase)], axis=1)
    factor = jnp.linalg.cholesky(jnp.dot(basis.T, basis, precision=HIGHEST))
    return (basis, factor)


def temporal_operator(pair_epochs, days):
    pinv = pseudo_inverse(pair_epochs)
    steps = jnp.concatenate(
        [jnp.zeros((1, pinv.shape[1]), jnp.float32), jnp.cumsum(pinv, axis=0)], axis=0
    )
    basis, factor = trend_basis(days)
    coefficients = jax.scipy.linalg.cho_solve(
        (factor, True), jnp.dot(basis.T, steps, precision=HIGHEST)
    )
    return steps - jnp.dot(basis, coefficients, precision=HIGHEST)


def window(start, length, extent, align):
    low = max(0, (start - RADIUS) // align * align)
    high = min(extent, -(-(start + length + RADIUS) // align) * align)
    return low, high


def tap_sum():
    return sum(jnp.exp(jnp.float32(-(i * i) / 8.0)) for i in range(-RADIUS, RADIUS + 1))


def band(shape, along, offset):
    one = lax.broadcasted_iota(jnp.int32, shape, along) + offset
    other = lax.broadcasted_iota(jnp.int32, shape, 1 - along)
    apart = one - other
    far = apart.astype(jnp.float32)
    weights = jnp.exp(far * far * -0.125) / tap_sum()
    return jnp.where(jnp.abs(apart) <= RADIUS, weights, 0.0)


def smooth_body(rows, cols, x_ref, out_ref, mid_ref):
    height, width = x_ref.shape[1:]
    n_quad = width // cols
    tall = min(256, height)
    wide = min(256, cols)
    bands = {}

    def banded(shape, along, offset):
        key = (shape, along, offset)
        if key not in bands:
            bands[key] = band(shape, along, offset)
        return bands[key]

    for r0 in range(0, height, tall):
        low, high = window(r0, tall, height, SUB)
        weights = banded((tall, high - low), 0, r0 - low)
        mid_ref[r0 : r0 + tall, :] = jnp.dot(
            weights, x_ref[0, low:high, :], precision=HIGHEST, preferred_element_type=jnp.float32
        )
    for c0 in range(0, width, wide):
        low, high = window(c0, wide, width, LANE)
        weights = banded((high - low, wide), 1, c0 - low)
        done = jnp.dot(
            mid_ref[:, low:high], weights, precision=HIGHEST, preferred_element_type=jnp.float32
        )
        quad, at = c0 // cols, c0 % cols
        for block in range(height // rows):
            out_ref[block * n_quad + quad, :, at : at + wide] = done[
                block * rows : (block + 1) * rows, :
            ]


def smooth_pair(interferograms, index, rows, cols):
    height, width = interferograms.shape[1:]
    blocks = (height // rows) * (width // cols)
    return pl.pallas_call(
        functools.partial(smooth_body, rows, cols),
        grid=(1,),
        in_specs=[pl.BlockSpec((1, height, width), lambda i: (index, 0, 0))],
        out_specs=pl.BlockSpec((blocks, rows, cols), lambda i: (0, 0, 0)),
        out_shape=jax.ShapeDtypeStruct((blocks, rows, cols), jnp.float32),
        scratch_shapes=[pltpu.VMEM((height, width), jnp.float32)],
        cost_estimate=pl.CostEstimate(
            flops=2 * height * width * 6 * 768,
            bytes_accessed=8 * height * width,
            transcendentals=0,
        ),
        name="smooth",
    )(interferograms)


def apply_body(n_in, has_acc, *refs):
    w_refs, x_refs = refs[:n_in], refs[n_in : 2 * n_in]
    out_ref = refs[-1]
    cols = out_ref.shape[-1]
    total = None
    for w_ref, x_ref in zip(w_refs, x_refs):
        x = x_ref[...].reshape(-1, cols)
        part = jnp.dot(w_ref[...], x, precision=HIGHEST, preferred_element_type=jnp.float32)
        total = part if total is None else total + part
    total = total.reshape(out_ref.shape)
    if has_acc:
        total = total + refs[2 * n_in][...]
    out_ref[...] = total


def apply_operator(weights, stacks, acc):
    pairs, rows, cols = stacks[0].shape
    epochs = weights[0].shape[0] // SUB
    n_in = len(stacks)
    moving = pl.BlockSpec((pairs, SUB, cols), lambda i: (0, i, 0))
    fixed = pl.BlockSpec((epochs * SUB, pairs * SUB), lambda i: (0, 0))
    out_spec = pl.BlockSpec((epochs, SUB, cols), lambda i: (0, i, 0))
    extra = [] if acc is None else [acc]
    return pl.pallas_call(
        functools.partial(apply_body, n_in, acc is not None),
        grid=(rows // SUB,),
        in_specs=[fixed] * n_in + [moving] * n_in + [out_spec] * len(extra),
        out_specs=out_spec,
        out_shape=jax.ShapeDtypeStruct((epochs, rows, cols), jnp.float32),
        cost_estimate=pl.CostEstimate(
            flops=2 * 6 * SUB * epochs * pairs * rows * cols * n_in,
            bytes_accessed=4 * rows * cols * (pairs * n_in + epochs),
            transcendentals=0,
        ),
        name="apply",
    )(*weights, *stacks, *extra)


def shards(interferograms, pair_epochs, days):
    n_pair = lax.axis_size("pair")
    n_quad = lax.axis_size("quad")
    local, height, width = interferograms.shape
    rows = height // n_pair
    cols = width // n_quad
    stacks = []
    for index in range(local):
        blocks = smooth_pair(interferograms, index, rows, cols)
        stacks.append(
            lax.all_to_all(blocks, ("pair", "quad"), split_axis=0, concat_axis=0, tiled=True)
        )
    operator = temporal_operator(pair_epochs, days)
    eye = jnp.eye(SUB, dtype=jnp.float32)
    weights = []
    for index in range(local):
        part = operator[:, index::local]
        spread = part[:, None, :, None] * eye[None, :, None, :]
        weights.append(spread.reshape(E * SUB, -1))
    total = None
    if local > 1:
        total = apply_operator(weights[:-1], stacks[:-1], None)
    return apply_operator(weights[-1:], stacks[-1:], total)


def solution(mesh):
    placed = (P(("pair", "quad"), "slab", None), P(), P())
    return jax.shard_map(
        shards,
        mesh=mesh,
        in_specs=placed,
        out_specs=P(None, ("slab", "pair"), "quad"),
        check_vma=False,
    )
```

```python
import functools

import jax
import jax.numpy as jnp
from jax import lax
from jax.experimental import pallas as pl
from jax.experimental.pallas import tpu as pltpu
from jax.sharding import PartitionSpec as P


E = 32
RADIUS = 6
SUB = 8
LANE = 128
HALO = 8
WIDE = 256
PARTS = 3
TERMS = ((0, 0), (0, 1), (1, 0), (1, 1), (0, 2), (2, 0))
HIGHEST = lax.Precision.HIGHEST
AXES = ("pair", "quad")

VMEM_LIMIT = 16 << 20


def pseudo_inverse(pair_epochs):
    first = pair_epochs[0]
    second = pair_epochs[1]
    steps_idx = jnp.arange(E - 1)
    design = (
        (first[:, None] <= steps_idx[None, :]) & (steps_idx[None, :] < second[:, None])
    ).astype(jnp.float32)
    normal = jnp.dot(design.T, design, precision=HIGHEST)
    factor = jnp.linalg.cholesky(normal)
    return jax.scipy.linalg.cho_solve((factor, True), design.T)


def trend_basis(days):
    times = days.astype(jnp.float32)
    scaled = (times - jnp.mean(times)) / 365.25
    phase = 2.0 * jnp.pi * times / 365.25
    basis = jnp.stack([jnp.ones_like(times), scaled, jnp.sin(phase), jnp.cos(phase)], axis=1)
    factor = jnp.linalg.cholesky(jnp.dot(basis.T, basis, precision=HIGHEST))
    return (basis, factor)


def temporal_operator(pair_epochs, days):
    pinv = pseudo_inverse(pair_epochs)
    steps = jnp.concatenate(
        [jnp.zeros((1, pinv.shape[1]), jnp.float32), jnp.cumsum(pinv, axis=0)], axis=0
    )
    basis, factor = trend_basis(days)
    coefficients = jax.scipy.linalg.cho_solve(
        (factor, True), jnp.dot(basis.T, steps, precision=HIGHEST)
    )
    return steps - jnp.dot(basis, coefficients, precision=HIGHEST)


def split(x):
    parts = []
    for _ in range(PARTS):
        part = x.astype(jnp.bfloat16)
        parts.append(part)
        x = x - part.astype(jnp.float32)
    return parts


def taps_at(apart):
    far = apart.astype(jnp.float32)
    total = sum(jnp.exp(jnp.float32(-(i * i) / 8.0)) for i in range(-RADIUS, RADIUS + 1))
    return jnp.where(jnp.abs(apart) <= RADIUS, jnp.exp(far * far * -0.125) / total, 0.0)


def choose(index, parts):
    out = parts[0]
    for k in range(1, len(parts)):
        out = jnp.where(index == k, parts[k], out)
    return out


def term_part(index, side):
    out = jnp.zeros_like(index)
    for k, term in enumerate(TERMS):
        out = jnp.where(index == k, term[side], out)
    return out


def smooth_body(mask, make_band, rows, cols, x_hbm, *refs):
    n_quad = lax.axis_size("quad")
    pair, quad = lax.axis_index("pair"), lax.axis_index("quad")
    local, height, width = x_hbm.shape
    if make_band:
        out_refs, band_ref, token_ref = refs[:n_quad], refs[n_quad], refs[n_quad + 1]
    else:
        band_ref, out_refs, token_ref = refs[0], refs[2 : 2 + n_quad], refs[2 + n_quad]
    xbuf, mid, sem = refs[-3:]
    token_ref[...] = jnp.zeros_like(token_ref)
    reach = xbuf.shape[1]
    high = local * rows
    row0 = lax.bitwise_xor(pair, mask) * rows
    low = pl.multiple_of(jnp.clip(row0 - HALO, 0, height - reach), SUB)
    copy = pltpu.make_async_copy(x_hbm.at[:, pl.ds(low, reach), :], xbuf, sem)
    copy.start()
    if make_band:
        shape = (WIDE + 2 * LANE, WIDE)
        apart = (
            lax.broadcasted_iota(jnp.int32, shape, 1)
            + LANE
            - lax.broadcasted_iota(jnp.int32, shape, 0)
        )
        for k, part in enumerate(split(taps_at(apart))):
            band_ref[k] = part
    shape = (rows, len(TERMS) * reach)
    at = lax.broadcasted_iota(jnp.int32, shape, 1)
    term = at // reach
    apart = lax.broadcasted_iota(jnp.int32, shape, 0) + (row0 - low) - (at - term * reach)
    parts = [part.astype(jnp.float32) for part in split(taps_at(apart))]
    row_band = choose(term_part(term, 0), parts).astype(jnp.bfloat16)
    edge = jnp.zeros((PARTS * high, LANE), jnp.bfloat16)
    mid[:, 0:LANE] = edge
    mid[:, LANE + width : 2 * LANE + width] = edge
    copy.wait()
    for p in range(local):
        parts = split(xbuf[p])
        tall = jnp.concatenate([parts[t[1]] for t in TERMS], axis=0)
        done = jnp.dot(row_band, tall, preferred_element_type=jnp.float32)
        for k, part in enumerate(split(done)):
            mid[k * high + p * rows : k * high + (p + 1) * rows, LANE : LANE + width] = part
    for flip in range(n_quad):
        for at in range(0, cols, WIDE):
            start = pl.multiple_of(lax.bitwise_xor(quad, flip) * cols + at, LANE)
            total = None
            for k in reversed(range(PARTS)):
                some = mid[0 : (PARTS - k) * high, pl.ds(start, WIDE + 2 * LANE)]
                done = jnp.dot(some, band_ref[k], preferred_element_type=jnp.float32)
                for j in reversed(range(PARTS - k)):
                    piece = done[j * high : (j + 1) * high]
                    total = piece if total is None else total + piece
            out_refs[flip][:, :, at : at + WIDE] = total.reshape(local, rows, WIDE)


def smooth_rows(interferograms, mask, band, token, rows, cols):
    local, height, width = interferograms.shape
    n_quad = width // cols
    reach = min(height, rows + 2 * HALO)
    vmem = pl.BlockSpec(memory_space=pltpu.VMEM)
    blocks = [jax.ShapeDtypeStruct((local, rows, cols), jnp.float32)] * n_quad
    band_shape = jax.ShapeDtypeStruct((PARTS, WIDE + 2 * LANE, WIDE), jnp.bfloat16)
    token_shape = jax.ShapeDtypeStruct((SUB, LANE), jnp.float32)
    make_band = band is None
    out = pl.pallas_call(
        functools.partial(smooth_body, mask, make_band, rows, cols),
        in_specs=[pl.BlockSpec(memory_space=pltpu.HBM)] + ([] if make_band else [vmem, vmem]),
        out_specs=[vmem] * (n_quad + make_band + 1),
        out_shape=blocks + [band_shape] * make_band + [token_shape],
        scratch_shapes=[
            pltpu.VMEM((local, reach, width), jnp.float32),
            pltpu.VMEM((PARTS * local * rows, width + 2 * LANE), jnp.bfloat16),
            pltpu.SemaphoreType.DMA(()),
        ],
        cost_estimate=pl.CostEstimate(
            flops=2 * local * rows * width * 6 * 768,
            bytes_accessed=4 * local * (rows + reach) * width,
            transcendentals=0,
        ),
        compiler_params=pltpu.CompilerParams(vmem_limit_bytes=VMEM_LIMIT),
    )(pltpu.with_memory_space_constraint(interferograms, pltpu.HBM), *([] if make_band else [band, token]))
    return out[:n_quad], (out[n_quad] if make_band else band), out[-1]


def expand_body(masks, local, op_ref, out_ref):
    n_quad = lax.axis_size("quad")
    me = lax.axis_index("pair") * n_quad + lax.axis_index("quad")
    tall, broad = out_ref.shape
    pairs = op_ref.shape[1]
    depth = len(masks) * local * SUB
    shape = (tall, E)
    repeat = (
        lax.broadcasted_iota(jnp.int32, shape, 0) // SUB
        == lax.broadcasted_iota(jnp.int32, shape, 1)
    ).astype(jnp.float32)
    shape = (pairs, broad)
    at = lax.broadcasted_iota(jnp.int32, shape, 1) % depth
    block = at // (local * SUB)
    mask = jnp.zeros_like(block)
    for k, value in enumerate(masks):
        mask = jnp.where(block == k, value, mask)
    source = lax.bitwise_xor(me, mask) * local + (at // SUB) % local
    place = (source == lax.broadcasted_iota(jnp.int32, shape, 0)).astype(jnp.float32)
    both = jnp.dot(repeat, op_ref[...], precision=HIGHEST, preferred_element_type=jnp.float32)
    both = jnp.dot(both, place, precision=HIGHEST, preferred_element_type=jnp.float32)
    shape = (tall, broad)
    at = lax.broadcasted_iota(jnp.int32, shape, 1)
    same = at % SUB == lax.broadcasted_iota(jnp.int32, shape, 0) % SUB
    parts = [part.astype(jnp.float32) for part in split(jnp.where(same, both, 0.0))]
    out_ref[...] = choose(term_part(at // depth, 0), parts).astype(jnp.bfloat16)


def expand(operator, masks, local):
    depth = len(masks) * local * SUB
    return pl.pallas_call(
        functools.partial(expand_body, masks, local),
        in_specs=[pl.BlockSpec(memory_space=pltpu.VMEM)],
        out_specs=pl.BlockSpec(memory_space=pltpu.VMEM),
        out_shape=jax.ShapeDtypeStruct((E * SUB, len(TERMS) * depth), jnp.bfloat16),
        compiler_params=pltpu.CompilerParams(vmem_limit_bytes=VMEM_LIMIT),
    )(operator)


def apply_body(n_in, has_acc, w_ref, *refs):
    x_refs, out_ref = refs[:n_in], refs[-1]
    cols = out_ref.shape[-1]
    x = jnp.concatenate([ref[...].reshape(-1, cols) for ref in x_refs], axis=0)
    parts = split(x)
    tall = jnp.concatenate([parts[t[1]] for t in TERMS], axis=0)
    total = jnp.dot(w_ref[...], tall, preferred_element_type=jnp.float32)
    total = total.reshape(out_ref.shape)
    if has_acc:
        total = total + refs[n_in][...]
    out_ref[...] = total


def apply_operator(weights, stacks, acc):
    local, rows, cols = stacks[0].shape
    n_in = len(stacks)
    moving = pl.BlockSpec((local, SUB, cols), lambda i: (0, i, 0))
    fixed = pl.BlockSpec(weights.shape, lambda i: (0, 0))
    out_spec = pl.BlockSpec((E, SUB, cols), lambda i: (0, i, 0))
    extra = [] if acc is None else [acc]
    return pl.pallas_call(
        functools.partial(apply_body, n_in, acc is not None),
        grid=(rows // SUB,),
        in_specs=[fixed] + [moving] * n_in + [out_spec] * len(extra),
        out_specs=out_spec,
        out_shape=jax.ShapeDtypeStruct((E, rows, cols), jnp.float32),
        cost_estimate=pl.CostEstimate(
            flops=2 * 6 * SUB * E * local * rows * cols * n_in,
            bytes_accessed=4 * rows * cols * (local * n_in + E),
            transcendentals=0,
        ),
        compiler_params=pltpu.CompilerParams(vmem_limit_bytes=VMEM_LIMIT),
    )(weights, *stacks, *extra)


def apply_last_body(n_in, w_ref, *refs):
    x_refs, acc_ref, out_hbm, buf, sems = refs[:n_in], *refs[n_in:]
    cols = out_hbm.shape[-1]
    copies = []
    for at in range(buf.shape[0]):
        span = pl.ds(at * SUB, SUB)
        x = jnp.concatenate([ref[:, span, :].reshape(-1, cols) for ref in x_refs], axis=0)
        parts = split(x)
        tall = jnp.concatenate([parts[t[1]] for t in TERMS], axis=0)
        total = jnp.dot(w_ref[...], tall, preferred_element_type=jnp.float32)
        buf[at] = total.reshape(buf.shape[1:]) + acc_ref[:, span, :]
        copies.append(pltpu.make_async_copy(buf.at[at], out_hbm.at[:, span, :], sems.at[at]))
        copies[-1].start()
    for copy in copies:
        copy.wait()


def apply_last(weights, stacks, acc):
    local, rows, cols = stacks[0].shape
    n_in = len(stacks)
    vmem = pl.BlockSpec(memory_space=pltpu.VMEM)
    return pl.pallas_call(
        functools.partial(apply_last_body, n_in),
        in_specs=[vmem] * (n_in + 2),
        out_specs=pl.BlockSpec(memory_space=pltpu.HBM),
        out_shape=jax.ShapeDtypeStruct((E, rows, cols), jnp.float32),
        scratch_shapes=[
            pltpu.VMEM((rows // SUB, E, SUB, cols), jnp.float32),
            pltpu.SemaphoreType.DMA((rows // SUB,)),
        ],
        cost_estimate=pl.CostEstimate(
            flops=2 * 6 * SUB * E * local * rows * cols * n_in,
            bytes_accessed=4 * rows * cols * (local * n_in + 2 * E),
            transcendentals=0,
        ),
        compiler_params=pltpu.CompilerParams(vmem_limit_bytes=VMEM_LIMIT),
        name="apply_last",
    )(weights, *stacks, acc)


def block_order(n_pair):
    far = list(range(n_pair // 2, n_pair))
    near = list(range(n_pair // 4, n_pair // 2))
    rest = list(range(n_pair // 4))[::-1]
    half = len(far) // 2
    return far[:half], near, far[half:], rest


def shards(interferograms, pair_epochs, days):
    n_pair = lax.axis_size("pair")
    n_quad = lax.axis_size("quad")
    local, height, width = interferograms.shape
    rows = height // n_pair
    cols = width // n_quad
    devices = n_pair * n_quad
    band, token, held = None, None, {}
    early, near, late, rest = block_order(n_pair)
    for mask in early + near + late + rest:
        blocks, band, token = smooth_rows(interferograms, mask, band, token, rows, cols)
        for flip, block in enumerate(blocks):
            which = mask * n_quad + flip
            if which:
                route = [(i, i ^ which) for i in range(devices)]
                block = lax.ppermute(block, AXES, route)
            held[which] = block
    operator = temporal_operator(pair_epochs, days)
    by_device = [
        [mask * n_quad + flip for mask in group for flip in range(n_quad)]
        for group in (rest[::-1] + early, near, late)
    ]
    stages, left = by_device[:2], by_device[2]
    floor = max(1, 16 // (local * SUB))
    while left:
        take = max(floor, len(left) // 2)
        stages.append(left[:take])
        left = left[take:]
    total = None
    for k, stage in enumerate(stages):
        weights = expand(operator, stage, local)
        stacks = [held[which] for which in stage]
        if k + 1 < len(stages):
            total = apply_operator(weights, stacks, total)
        else:
            total = apply_last(weights, stacks, total)
    return total


def solution(mesh):
    placed = (P(("pair", "quad"), "slab", None), P(), P())

    return jax.shard_map(
        shards,
        mesh=mesh,
        in_specs=placed,
        out_specs=P(None, ("slab", "pair"), "quad"),
        check_vma=False,
    )
```

```python
import functools

import jax
import jax.numpy as jnp
from jax import lax
from jax.experimental import pallas as pl
from jax.experimental.pallas import tpu as pltpu
from jax.sharding import PartitionSpec as P


E = 32
TREND = 4
RADIUS = 6
SUB = 8
LANE = 128
HALO = 8
WIDE = 256
PARTS = 3
TERMS = ((0, 0), (0, 1), (1, 0), (1, 1), (0, 2), (2, 0))
HIGHEST = lax.Precision.HIGHEST
AXES = ("pair", "quad")

VMEM_LIMIT = 16 << 20


def operator_body(epochs_ref, days_ref, whole_ref, narrow_ref, basis_ref):
    epochs = epochs_ref[...]
    at = lax.broadcasted_iota(jnp.int32, (E, epochs.shape[1]), 0)
    design = ((epochs[0:1, :] <= at) & (at < epochs[1:2, :])).astype(jnp.float32)
    row = lax.broadcasted_iota(jnp.int32, (E, E), 0)
    lane = lax.broadcasted_iota(jnp.int32, (E, E), 1)
    rows = lax.broadcasted_iota(jnp.int32, (E, 1), 0)
    normal = lax.dot_general(
        design, design, (((1,), (1,)), ((), ())), preferred_element_type=jnp.float32
    )
    normal = jnp.where((row == E - 1) & (lane == E - 1), 1.0, normal)
    solved = design
    for i in range(E - 1):
        inverse = 1.0 / normal[i : i + 1, i : i + 1]
        factor = normal[:, i : i + 1]
        factor = jnp.where(rows == i, factor - 1.0, factor)
        lead = normal[i : i + 1, :] * inverse
        other = solved[i : i + 1, :] * inverse
        normal = normal - factor * lead
        solved = solved - factor * other
    below = (lane < row).astype(jnp.float32)
    steps = jnp.dot(below, solved, precision=HIGHEST, preferred_element_type=jnp.float32)
    days = jnp.broadcast_to(days_ref[...].astype(jnp.float32), (E, E))
    times = jnp.sum(jnp.where(row == lane, days, 0.0), axis=1, keepdims=True)
    scaled = (times - jnp.sum(times, axis=0, keepdims=True) / E) / 365.25
    phase = 2.0 * jnp.pi * times / 365.25
    trend = choose(
        lane, [jnp.ones_like(days), scaled, jnp.sin(phase), jnp.cos(phase), jnp.zeros_like(days)]
    )
    turn = (row == lane).astype(jnp.float32)
    for j in range(TREND):
        v = jnp.where(rows >= j, trend[:, j : j + 1], 0.0)
        norm = jnp.sqrt(jnp.sum(v * v, axis=0, keepdims=True))
        head = trend[j : j + 1, j : j + 1]
        v = v + jnp.where(rows == j, jnp.where(head >= 0.0, norm, -norm), 0.0)
        w = v * (2.0 / jnp.sum(v * v, axis=0, keepdims=True))
        trend = trend - w * jnp.sum(v * trend, axis=0, keepdims=True)
        turn = turn - w * jnp.sum(v * turn, axis=0, keepdims=True)
        steps = steps - w * jnp.sum(v * steps, axis=0, keepdims=True)
    shape = (E, E - TREND)
    keep = (
        lax.broadcasted_iota(jnp.int32, shape, 0)
        == lax.broadcasted_iota(jnp.int32, shape, 1) + TREND
    ).astype(jnp.float32)
    basis = jnp.dot(turn.T, keep, precision=HIGHEST, preferred_element_type=jnp.float32)
    narrow = steps[TREND:, :]
    basis_ref[...] = basis
    narrow_ref[...] = narrow
    whole_ref[...] = jnp.dot(basis, narrow, precision=HIGHEST, preferred_element_type=jnp.float32)


def temporal_operator(pair_epochs, days):
    pairs = pair_epochs.shape[1]
    vmem = pl.BlockSpec(memory_space=pltpu.VMEM)
    shapes = [(E, pairs), (E - TREND, pairs), (E, E - TREND)]
    return pl.pallas_call(
        operator_body,
        in_specs=[vmem] * 2,
        out_specs=[vmem] * 3,
        out_shape=[jax.ShapeDtypeStruct(shape, jnp.float32) for shape in shapes],
        compiler_params=pltpu.CompilerParams(vmem_limit_bytes=VMEM_LIMIT),
        name="operator",
    )(pair_epochs, days.reshape(1, E))


def split(x):
    parts = []
    for _ in range(PARTS):
        part = x.astype(jnp.bfloat16)
        parts.append(part)
        x = x - part.astype(jnp.float32)
    return parts


def taps_at(apart):
    far = apart.astype(jnp.float32)
    total = sum(jnp.exp(jnp.float32(-(i * i) / 8.0)) for i in range(-RADIUS, RADIUS + 1))
    return jnp.where(jnp.abs(apart) <= RADIUS, jnp.exp(far * far * -0.125) / total, 0.0)


def choose(index, parts):
    out = parts[0]
    for k in range(1, len(parts)):
        out = jnp.where(index == k, parts[k], out)
    return out


def term_part(index, side):
    out = jnp.zeros_like(index)
    for k, term in enumerate(TERMS):
        out = jnp.where(index == k, term[side], out)
    return out


def smooth_body(mask, make_band, rows, cols, cuts, x_hbm, *refs):
    n_quad = lax.axis_size("quad")
    pair, quad = lax.axis_index("pair"), lax.axis_index("quad")
    local, height, width = x_hbm.shape
    n_out = n_quad * len(cuts)
    if make_band:
        out_refs, band_ref, token_ref = refs[:n_out], refs[n_out], refs[n_out + 1]
    else:
        band_ref, out_refs, token_ref = refs[0], refs[2 : 2 + n_out], refs[2 + n_out]
    xbuf, mid, sems = refs[-3:]
    token_ref[...] = jnp.zeros_like(token_ref)
    reach = xbuf.shape[1]
    high = local * rows
    row0 = lax.bitwise_xor(pair, mask) * rows
    low = pl.multiple_of(jnp.clip(row0 - HALO, 0, height - reach), SUB)
    copies = [
        pltpu.make_async_copy(x_hbm.at[p, pl.ds(low, reach), :], xbuf.at[p], sems.at[p])
        for p in range(local)
    ]
    for copy in copies:
        copy.start()
    if make_band:
        shape = (WIDE + 2 * LANE, WIDE)
        apart = (
            lax.broadcasted_iota(jnp.int32, shape, 1)
            + LANE
            - lax.broadcasted_iota(jnp.int32, shape, 0)
        )
        for k, part in enumerate(split(taps_at(apart))):
            band_ref[k] = part
    shape = (rows, len(TERMS) * reach)
    at = lax.broadcasted_iota(jnp.int32, shape, 1)
    term = at // reach
    apart = lax.broadcasted_iota(jnp.int32, shape, 0) + (row0 - low) - (at - term * reach)
    parts = [part.astype(jnp.float32) for part in split(taps_at(apart))]
    row_band = choose(term_part(term, 0), parts).astype(jnp.bfloat16)
    edge = jnp.zeros((PARTS * high, LANE), jnp.bfloat16)
    mid[:, 0:LANE] = edge
    mid[:, LANE + width : 2 * LANE + width] = edge
    for p in range(local):
        copies[p].wait()
        parts = split(xbuf[p])
        tall = jnp.concatenate([parts[t[1]] for t in TERMS], axis=0)
        done = jnp.dot(row_band, tall, preferred_element_type=jnp.float32)
        for k, part in enumerate(split(done)):
            mid[k * high + p * rows : k * high + (p + 1) * rows, LANE : LANE + width] = part
    for flip in range(n_quad):
        for at in range(0, cols, WIDE):
            start = pl.multiple_of(lax.bitwise_xor(quad, flip) * cols + at, LANE)
            total = None
            for k in reversed(range(PARTS)):
                some = mid[0 : (PARTS - k) * high, pl.ds(start, WIDE + 2 * LANE)]
                done = jnp.dot(some, band_ref[k], preferred_element_type=jnp.float32)
                for j in reversed(range(PARTS - k)):
                    piece = done[j * high : (j + 1) * high]
                    total = piece if total is None else total + piece
            total = total.reshape(local, rows, WIDE)
            top = 0
            for k, size in enumerate(cuts):
                out_ref = out_refs[flip * len(cuts) + k]
                out_ref[:, :, at : at + WIDE] = total[:, top : top + size]
                top += size


def smooth_rows(interferograms, mask, band, token, rows, cols, cuts):
    local, height, width = interferograms.shape
    n_quad = width // cols
    reach = min(height, rows + 2 * HALO)
    vmem = pl.BlockSpec(memory_space=pltpu.VMEM)
    blocks = [jax.ShapeDtypeStruct((local, size, cols), jnp.float32) for size in cuts] * n_quad
    band_shape = jax.ShapeDtypeStruct((PARTS, WIDE + 2 * LANE, WIDE), jnp.bfloat16)
    token_shape = jax.ShapeDtypeStruct((SUB, LANE), jnp.float32)
    make_band = band is None
    where = pl.BlockSpec(memory_space=pltpu.HBM if make_band else pl.ANY)
    if make_band:
        interferograms = pltpu.with_memory_space_constraint(interferograms, pltpu.HBM)
    out = pl.pallas_call(
        functools.partial(smooth_body, mask, make_band, rows, cols, cuts),
        in_specs=[where] + ([] if make_band else [vmem, vmem]),
        out_specs=[vmem] * (len(blocks) + make_band + 1),
        out_shape=blocks + [band_shape] * make_band + [token_shape],
        scratch_shapes=[
            pltpu.VMEM((local, reach, width), jnp.float32),
            pltpu.VMEM((PARTS * local * rows, width + 2 * LANE), jnp.bfloat16),
            pltpu.SemaphoreType.DMA((local,)),
        ],
        cost_estimate=pl.CostEstimate(
            flops=2 * local * rows * width * 6 * 768,
            bytes_accessed=4 * local * (rows + reach) * width,
            transcendentals=0,
        ),
        compiler_params=pltpu.CompilerParams(vmem_limit_bytes=VMEM_LIMIT),
    )(interferograms, *([] if make_band else [band, token]))
    n_cuts = len(cuts)
    blocks = [out[flip * n_cuts : (flip + 1) * n_cuts] for flip in range(n_quad)]
    return blocks, (out[len(blocks) * n_cuts] if make_band else band), out[-1]


def expand_body(masks, local, op_ref, out_ref):
    n_quad = lax.axis_size("quad")
    me = lax.axis_index("pair") * n_quad + lax.axis_index("quad")
    tall, broad = out_ref.shape
    lines, pairs = op_ref.shape
    depth = broad // len(TERMS)
    shape = (tall, lines)
    repeat = (
        lax.broadcasted_iota(jnp.int32, shape, 0) // SUB
        == lax.broadcasted_iota(jnp.int32, shape, 1)
    ).astype(jnp.float32)
    shape = (pairs, broad)
    at = lax.broadcasted_iota(jnp.int32, shape, 1) % depth
    source = at // SUB
    if masks is not None:
        block = source // local
        mask = jnp.zeros_like(block)
        for k, value in enumerate(masks):
            mask = jnp.where(block == k, value, mask)
        source = lax.bitwise_xor(me, mask) * local + source % local
    place = (source == lax.broadcasted_iota(jnp.int32, shape, 0)).astype(jnp.float32)
    both = jnp.dot(repeat, op_ref[...], precision=HIGHEST, preferred_element_type=jnp.float32)
    both = jnp.dot(both, place, precision=HIGHEST, preferred_element_type=jnp.float32)
    shape = (tall, broad)
    at = lax.broadcasted_iota(jnp.int32, shape, 1)
    same = at % SUB == lax.broadcasted_iota(jnp.int32, shape, 0) % SUB
    parts = [part.astype(jnp.float32) for part in split(jnp.where(same, both, 0.0))]
    out_ref[...] = choose(term_part(at // depth, 0), parts).astype(jnp.bfloat16)


def expand(operator, masks, local):
    lines, pairs = operator.shape
    depth = (pairs if masks is None else len(masks) * local) * SUB
    return pl.pallas_call(
        functools.partial(expand_body, masks, local),
        in_specs=[pl.BlockSpec(memory_space=pltpu.VMEM)],
        out_specs=pl.BlockSpec(memory_space=pltpu.VMEM),
        out_shape=jax.ShapeDtypeStruct((lines * SUB, len(TERMS) * depth), jnp.bfloat16),
        compiler_params=pltpu.CompilerParams(vmem_limit_bytes=VMEM_LIMIT),
    )(operator)


def product(weights, stacks, at):
    span = pl.ds(at, SUB)
    x = jnp.concatenate([ref[:, span, :].reshape(-1, ref.shape[2]) for ref in stacks], axis=0)
    parts = split(x)
    tall = jnp.concatenate([parts[t[1]] for t in TERMS], axis=0)
    total = jnp.dot(weights, tall, preferred_element_type=jnp.float32)
    return total.reshape(-1, SUB, total.shape[1])


def apply_body(n_in, starts, has_acc, w_ref, *refs):
    x_refs, out_ref = refs[:n_in], refs[-1]
    for k, at in enumerate(starts):
        total = product(w_ref[...], x_refs, at)
        if has_acc:
            total = total + refs[n_in][:, pl.ds(k * SUB, SUB), :]
        out_ref[:, pl.ds(k * SUB, SUB), :] = total


def apply_operator(weights, stacks, acc, starts):
    cols = stacks[0].shape[2]
    lines = weights.shape[0] // SUB
    vmem = pl.BlockSpec(memory_space=pltpu.VMEM)
    extra = [] if acc is None else [acc]
    count = len(starts) * SUB
    return pl.pallas_call(
        functools.partial(apply_body, len(stacks), starts, acc is not None),
        in_specs=[vmem] * (1 + len(stacks) + len(extra)),
        out_specs=vmem,
        out_shape=jax.ShapeDtypeStruct((lines, count, cols), jnp.float32),
        cost_estimate=pl.CostEstimate(
            flops=2 * weights.shape[0] * weights.shape[1] * len(starts) * cols,
            bytes_accessed=4 * count * cols * (len(stacks) * stacks[0].shape[0] + lines),
            transcendentals=0,
        ),
        compiler_params=pltpu.CompilerParams(vmem_limit_bytes=VMEM_LIMIT),
    )(weights, *stacks, *extra)


def finish_body(n_in, starts, top, skip, has_out, w_ref, *refs):
    x_refs, acc_ref = refs[:n_in], refs[n_in]
    out_hbm, buf, sems = refs[n_in + 1 + has_out :]
    copies = []
    for k, at in enumerate(starts):
        buf[k] = product(w_ref[...], x_refs, at) + acc_ref[:, pl.ds(skip + k * SUB, SUB), :]
        rows = pl.ds(top + k * SUB, SUB)
        copies.append(pltpu.make_async_copy(buf.at[k], out_hbm.at[:, rows, :], sems.at[k]))
        copies[-1].start()
    for copy in copies:
        copy.wait()


def finish(weights, stacks, acc, starts, top, skip, out, rows):
    cols = stacks[0].shape[2]
    n_in, count = len(stacks), len(starts)
    vmem = pl.BlockSpec(memory_space=pltpu.VMEM)
    hbm = pl.BlockSpec(memory_space=pltpu.HBM)
    extra = [] if out is None else [out]
    return pl.pallas_call(
        functools.partial(finish_body, n_in, starts, top, skip, len(extra)),
        in_specs=[vmem] * (n_in + 2) + [hbm] * len(extra),
        out_specs=hbm,
        out_shape=jax.ShapeDtypeStruct((E, rows, cols), jnp.float32),
        input_output_aliases={n_in + 2: 0} if extra else {},
        scratch_shapes=[
            pltpu.VMEM((count, E, SUB, cols), jnp.float32),
            pltpu.SemaphoreType.DMA((count,)),
        ],
        cost_estimate=pl.CostEstimate(
            flops=2 * weights.shape[0] * weights.shape[1] * count * cols,
            bytes_accessed=4 * count * SUB * cols * (n_in * stacks[0].shape[0] + 2 * E),
            transcendentals=0,
        ),
        compiler_params=pltpu.CompilerParams(vmem_limit_bytes=VMEM_LIMIT),
    )(weights, *stacks, acc, *extra)


class Plan:
    def __init__(self, n_pair, n_quad, rows):
        self.devices = n_pair * n_quad
        self.half = self.devices // 2
        far = list(range(n_pair // 2, n_pair))
        middle = len(far) // 2
        self.far = far[middle:] + far[:middle]
        near = list(range(n_pair // 4, n_pair // 2))
        self.near = near
        self.rest = list(range(n_pair // 4))[::-1]
        groups = rows // SUB
        self.merged = list(range(groups - max(1, groups // 2), groups))
        self.plain = list(range(self.merged[0]))
        self.split = self.merged[0] * SUB


def shards(interferograms, pair_epochs, days):
    n_pair = lax.axis_size("pair")
    n_quad = lax.axis_size("quad")
    local, height, width = interferograms.shape
    rows = height // n_pair
    cols = width // n_quad
    plan = Plan(n_pair, n_quad, rows)
    half = plan.half
    state = [None, None]

    def smooth(mask, cuts):
        blocks, state[0], state[1] = smooth_rows(
            interferograms, mask, *state, rows, cols, cuts
        )
        return blocks

    def send(block, which):
        if which == 0:
            return block
        route = [(i, i ^ which) for i in range(plan.devices)]
        return lax.ppermute(block, AXES, route)

    plain, gathered, own = {}, {}, {}
    for mask in plan.far:
        blocks = smooth(mask, (plan.split, rows - plan.split))
        for flip, (first, second) in enumerate(blocks):
            which = mask * n_quad + flip
            gathered[which - half] = send(second, which - half)
            plain[which] = send(first, which)
    whole, narrow, basis = temporal_operator(pair_epochs, days)
    everyone = list(range(half))
    weights = expand(narrow, everyone, local)
    arrived = []
    for k in range(len(plan.merged)):
        some = apply_operator(weights, [gathered[w] for w in everyone], None, [k * SUB])
        arrived.append(send(some, half))
    for mask in plan.near + plan.rest:
        for flip, (block,) in enumerate(smooth(mask, (rows,))):
            which = mask * n_quad + flip
            own[which] = send(block, which)
    total = None
    starts = [k * SUB for k in plan.plain]
    left = [mask * n_quad + flip for mask in plan.far for flip in range(n_quad)]
    weights = expand(whole, left, local)
    total = apply_operator(weights, [plain[w] for w in left], None, starts)
    weights = expand(whole, everyone, local)
    stacks = [own[w] for w in everyone]
    out = finish(weights, stacks, total, starts, 0, 0, None, rows)
    later = [k * SUB for k in plan.merged]
    total = apply_operator(weights, stacks, None, later)
    weights = expand(basis, None, local)
    for k, group in enumerate(plan.merged):
        top = group * SUB
        out = finish(weights, [arrived[k]], total, [0], top, k * SUB, out, rows)
    return out


def solution(mesh):
    placed = (P(("pair", "quad"), "slab", None), P(), P())

    def step(interferograms, pair_epochs, days):
        mapped = jax.shard_map(
            shards,
            mesh=mesh,
            in_specs=placed,
            out_specs=P(None, ("slab", "pair"), "quad"),
            check_vma=False,
        )
        return mapped(interferograms, pair_epochs, days)

    return step
```

```python
import functools

import jax
import jax.numpy as jnp
from jax import lax
from jax.experimental import pallas as pl
from jax.experimental.pallas import tpu as pltpu
from jax.sharding import PartitionSpec as P


E = 32
TREND = 4
RADIUS = 6
SUB = 8
LANE = 128
HALO = 8
WIDE = 256
PARTS = 3
TERMS = ((0, 0), (0, 1), (1, 0), (1, 1), (0, 2), (2, 0))
HIGHEST = lax.Precision.HIGHEST
AXES = ("pair", "quad")

VMEM_LIMIT = 16 << 20


def operator_body(epochs_ref, days_ref, whole_ref, narrow_ref, basis_ref):
    epochs = epochs_ref[...]
    at = lax.broadcasted_iota(jnp.int32, (E, epochs.shape[1]), 0)
    design = ((epochs[0:1, :] <= at) & (at < epochs[1:2, :])).astype(jnp.float32)
    row = lax.broadcasted_iota(jnp.int32, (E, E), 0)
    lane = lax.broadcasted_iota(jnp.int32, (E, E), 1)
    rows = lax.broadcasted_iota(jnp.int32, (E, 1), 0)
    normal = lax.dot_general(
        design, design, (((1,), (1,)), ((), ())), preferred_element_type=jnp.float32
    )
    normal = jnp.where((row == E - 1) & (lane == E - 1), 1.0, normal)
    solved = design
    for i in range(E - 1):
        inverse = 1.0 / normal[i : i + 1, i : i + 1]
        factor = normal[:, i : i + 1]
        factor = jnp.where(rows == i, factor - 1.0, factor)
        lead = normal[i : i + 1, :] * inverse
        other = solved[i : i + 1, :] * inverse
        normal = normal - factor * lead
        solved = solved - factor * other
    below = (lane < row).astype(jnp.float32)
    steps = jnp.dot(below, solved, precision=HIGHEST, preferred_element_type=jnp.float32)
    days = jnp.broadcast_to(days_ref[...].astype(jnp.float32), (E, E))
    times = jnp.sum(jnp.where(row == lane, days, 0.0), axis=1, keepdims=True)
    scaled = (times - jnp.sum(times, axis=0, keepdims=True) / E) / 365.25
    phase = 2.0 * jnp.pi * times / 365.25
    trend = choose(
        lane, [jnp.ones_like(days), scaled, jnp.sin(phase), jnp.cos(phase), jnp.zeros_like(days)]
    )
    turn = (row == lane).astype(jnp.float32)
    for j in range(TREND):
        v = jnp.where(rows >= j, trend[:, j : j + 1], 0.0)
        norm = jnp.sqrt(jnp.sum(v * v, axis=0, keepdims=True))
        head = trend[j : j + 1, j : j + 1]
        v = v + jnp.where(rows == j, jnp.where(head >= 0.0, norm, -norm), 0.0)
        w = v * (2.0 / jnp.sum(v * v, axis=0, keepdims=True))
        trend = trend - w * jnp.sum(v * trend, axis=0, keepdims=True)
        turn = turn - w * jnp.sum(v * turn, axis=0, keepdims=True)
        steps = steps - w * jnp.sum(v * steps, axis=0, keepdims=True)
    shape = (E, E - TREND)
    keep = (
        lax.broadcasted_iota(jnp.int32, shape, 0)
        == lax.broadcasted_iota(jnp.int32, shape, 1) + TREND
    ).astype(jnp.float32)
    basis = jnp.dot(turn.T, keep, precision=HIGHEST, preferred_element_type=jnp.float32)
    narrow = steps[TREND:, :]
    basis_ref[...] = basis
    narrow_ref[...] = narrow
    whole_ref[...] = jnp.dot(basis, narrow, precision=HIGHEST, preferred_element_type=jnp.float32)


def temporal_operator(pair_epochs, days):
    pairs = pair_epochs.shape[1]
    vmem = pl.BlockSpec(memory_space=pltpu.VMEM)
    shapes = [(E, pairs), (E - TREND, pairs), (E, E - TREND)]
    return pl.pallas_call(
        operator_body,
        in_specs=[vmem] * 2,
        out_specs=[vmem] * 3,
        out_shape=[jax.ShapeDtypeStruct(shape, jnp.float32) for shape in shapes],
        compiler_params=pltpu.CompilerParams(vmem_limit_bytes=VMEM_LIMIT),
        name="operator",
    )(pair_epochs, days.reshape(1, E))


def split(x):
    parts = []
    for _ in range(PARTS):
        part = x.astype(jnp.bfloat16)
        parts.append(part)
        x = x - part.astype(jnp.float32)
    return parts


def taps_at(apart):
    far = apart.astype(jnp.float32)
    total = sum(jnp.exp(jnp.float32(-(i * i) / 8.0)) for i in range(-RADIUS, RADIUS + 1))
    return jnp.where(jnp.abs(apart) <= RADIUS, jnp.exp(far * far * -0.125) / total, 0.0)


def choose(index, parts):
    out = parts[0]
    for k in range(1, len(parts)):
        out = jnp.where(index == k, parts[k], out)
    return out


def term_part(index, side):
    out = jnp.zeros_like(index)
    for k, term in enumerate(TERMS):
        out = jnp.where(index == k, term[side], out)
    return out


def smooth_body(mask, make_band, rows, cols, cuts, x_hbm, *refs):
    n_quad = lax.axis_size("quad")
    pair, quad = lax.axis_index("pair"), lax.axis_index("quad")
    local, height, width = x_hbm.shape
    n_out = n_quad * len(cuts)
    if make_band:
        out_refs, band_ref, token_ref = refs[:n_out], refs[n_out], refs[n_out + 1]
    else:
        band_ref, out_refs, token_ref = refs[0], refs[2 : 2 + n_out], refs[2 + n_out]
    xbuf, mid, sems = refs[-3:]
    token_ref[...] = jnp.zeros_like(token_ref)
    reach = xbuf.shape[1]
    high = local * rows
    row0 = lax.bitwise_xor(pair, mask) * rows
    low = pl.multiple_of(jnp.clip(row0 - HALO, 0, height - reach), SUB)
    copies = [
        pltpu.make_async_copy(x_hbm.at[p, pl.ds(low, reach), :], xbuf.at[p], sems.at[p])
        for p in range(local)
    ]
    for copy in copies:
        copy.start()
    if make_band:
        shape = (WIDE + 2 * LANE, WIDE)
        apart = (
            lax.broadcasted_iota(jnp.int32, shape, 1)
            + LANE
            - lax.broadcasted_iota(jnp.int32, shape, 0)
        )
        for k, part in enumerate(split(taps_at(apart))):
            band_ref[k] = part
    shape = (rows, len(TERMS) * reach)
    at = lax.broadcasted_iota(jnp.int32, shape, 1)
    term = at // reach
    apart = lax.broadcasted_iota(jnp.int32, shape, 0) + (row0 - low) - (at - term * reach)
    parts = [part.astype(jnp.float32) for part in split(taps_at(apart))]
    row_band = choose(term_part(term, 0), parts).astype(jnp.bfloat16)
    edge = jnp.zeros((PARTS * high, LANE), jnp.bfloat16)
    mid[:, 0:LANE] = edge
    mid[:, LANE + width : 2 * LANE + width] = edge
    for p in range(local):
        copies[p].wait()
        parts = split(xbuf[p])
        tall = jnp.concatenate([parts[t[1]] for t in TERMS], axis=0)
        done = jnp.dot(row_band, tall, preferred_element_type=jnp.float32)
        for k, part in enumerate(split(done)):
            mid[k * high + p * rows : k * high + (p + 1) * rows, LANE : LANE + width] = part
    for flip in range(n_quad):
        for at in range(0, cols, WIDE):
            start = pl.multiple_of(lax.bitwise_xor(quad, flip) * cols + at, LANE)
            total = None
            for k in reversed(range(PARTS)):
                some = mid[0 : (PARTS - k) * high, pl.ds(start, WIDE + 2 * LANE)]
                done = jnp.dot(some, band_ref[k], preferred_element_type=jnp.float32)
                for j in reversed(range(PARTS - k)):
                    piece = done[j * high : (j + 1) * high]
                    total = piece if total is None else total + piece
            total = total.reshape(local, rows, WIDE)
            top = 0
            for k, size in enumerate(cuts):
                out_ref = out_refs[flip * len(cuts) + k]
                out_ref[:, :, at : at + WIDE] = total[:, top : top + size]
                top += size


def smooth_rows(interferograms, mask, band, token, rows, cols, cuts):
    local, height, width = interferograms.shape
    n_quad = width // cols
    reach = min(height, rows + 2 * HALO)
    vmem = pl.BlockSpec(memory_space=pltpu.VMEM)
    blocks = [jax.ShapeDtypeStruct((local, size, cols), jnp.float32) for size in cuts] * n_quad
    band_shape = jax.ShapeDtypeStruct((PARTS, WIDE + 2 * LANE, WIDE), jnp.bfloat16)
    token_shape = jax.ShapeDtypeStruct((SUB, LANE), jnp.float32)
    make_band = band is None
    where = pl.BlockSpec(memory_space=pltpu.HBM if make_band else pl.ANY)
    if make_band:
        interferograms = pltpu.with_memory_space_constraint(interferograms, pltpu.HBM)
    out = pl.pallas_call(
        functools.partial(smooth_body, mask, make_band, rows, cols, cuts),
        in_specs=[where] + ([] if make_band else [vmem, vmem]),
        out_specs=[vmem] * (len(blocks) + make_band + 1),
        out_shape=blocks + [band_shape] * make_band + [token_shape],
        scratch_shapes=[
            pltpu.VMEM((local, reach, width), jnp.float32),
            pltpu.VMEM((PARTS * local * rows, width + 2 * LANE), jnp.bfloat16),
            pltpu.SemaphoreType.DMA((local,)),
        ],
        cost_estimate=pl.CostEstimate(
            flops=2 * local * rows * width * 6 * 768,
            bytes_accessed=4 * local * (rows + reach) * width,
            transcendentals=0,
        ),
        compiler_params=pltpu.CompilerParams(vmem_limit_bytes=VMEM_LIMIT),
    )(interferograms, *([] if make_band else [band, token]))
    n_cuts = len(cuts)
    blocks = [out[flip * n_cuts : (flip + 1) * n_cuts] for flip in range(n_quad)]
    return blocks, (out[len(blocks) * n_cuts] if make_band else band), out[-1]


def expand_body(masks, local, op_ref, out_ref):
    n_quad = lax.axis_size("quad")
    me = lax.axis_index("pair") * n_quad + lax.axis_index("quad")
    tall, broad = out_ref.shape
    lines, pairs = op_ref.shape
    depth = broad // len(TERMS)
    shape = (tall, lines)
    repeat = (
        lax.broadcasted_iota(jnp.int32, shape, 0) // SUB
        == lax.broadcasted_iota(jnp.int32, shape, 1)
    ).astype(jnp.float32)
    shape = (pairs, broad)
    at = lax.broadcasted_iota(jnp.int32, shape, 1) % depth
    source = at // SUB
    if masks is not None:
        block = source // local
        mask = jnp.zeros_like(block)
        for k, value in enumerate(masks):
            mask = jnp.where(block == k, value, mask)
        source = lax.bitwise_xor(me, mask) * local + source % local
    place = (source == lax.broadcasted_iota(jnp.int32, shape, 0)).astype(jnp.float32)
    both = jnp.dot(repeat, op_ref[...], precision=HIGHEST, preferred_element_type=jnp.float32)
    both = jnp.dot(both, place, precision=HIGHEST, preferred_element_type=jnp.float32)
    shape = (tall, broad)
    at = lax.broadcasted_iota(jnp.int32, shape, 1)
    same = at % SUB == lax.broadcasted_iota(jnp.int32, shape, 0) % SUB
    parts = [part.astype(jnp.float32) for part in split(jnp.where(same, both, 0.0))]
    out_ref[...] = choose(term_part(at // depth, 0), parts).astype(jnp.bfloat16)


def expand(operator, masks, local):
    lines, pairs = operator.shape
    depth = (pairs if masks is None else len(masks) * local) * SUB
    return pl.pallas_call(
        functools.partial(expand_body, masks, local),
        in_specs=[pl.BlockSpec(memory_space=pltpu.VMEM)],
        out_specs=pl.BlockSpec(memory_space=pltpu.VMEM),
        out_shape=jax.ShapeDtypeStruct((lines * SUB, len(TERMS) * depth), jnp.bfloat16),
        compiler_params=pltpu.CompilerParams(vmem_limit_bytes=VMEM_LIMIT),
    )(operator)


def product(weights, stacks, at):
    span = pl.ds(at, SUB)
    x = jnp.concatenate([ref[:, span, :].reshape(-1, ref.shape[2]) for ref in stacks], axis=0)
    parts = split(x)
    tall = jnp.concatenate([parts[t[1]] for t in TERMS], axis=0)
    total = jnp.dot(weights, tall, preferred_element_type=jnp.float32)
    return total.reshape(-1, SUB, total.shape[1])


def apply_body(n_in, starts, has_acc, w_ref, *refs):
    x_refs, out_ref = refs[:n_in], refs[-1]
    for k, at in enumerate(starts):
        total = product(w_ref[...], x_refs, at)
        if has_acc:
            total = total + refs[n_in][:, pl.ds(k * SUB, SUB), :]
        out_ref[:, pl.ds(k * SUB, SUB), :] = total


def apply_operator(weights, stacks, acc, starts):
    cols = stacks[0].shape[2]
    lines = weights.shape[0] // SUB
    vmem = pl.BlockSpec(memory_space=pltpu.VMEM)
    extra = [] if acc is None else [acc]
    count = len(starts) * SUB
    return pl.pallas_call(
        functools.partial(apply_body, len(stacks), starts, acc is not None),
        in_specs=[vmem] * (1 + len(stacks) + len(extra)),
        out_specs=vmem,
        out_shape=jax.ShapeDtypeStruct((lines, count, cols), jnp.float32),
        cost_estimate=pl.CostEstimate(
            flops=2 * weights.shape[0] * weights.shape[1] * len(starts) * cols,
            bytes_accessed=4 * count * cols * (len(stacks) * stacks[0].shape[0] + lines),
            transcendentals=0,
        ),
        compiler_params=pltpu.CompilerParams(vmem_limit_bytes=VMEM_LIMIT),
    )(weights, *stacks, *extra)


def finish_body(n_in, starts, top, skip, has_out, w_ref, *refs):
    x_refs, acc_ref = refs[:n_in], refs[n_in]
    out_hbm, buf, sems = refs[n_in + 1 + has_out :]
    copies = []
    for k, at in enumerate(starts):
        buf[k] = product(w_ref[...], x_refs, at) + acc_ref[:, pl.ds(skip + k * SUB, SUB), :]
        rows = pl.ds(top + k * SUB, SUB)
        copies.append(pltpu.make_async_copy(buf.at[k], out_hbm.at[:, rows, :], sems.at[k]))
        copies[-1].start()
    for copy in copies:
        copy.wait()


def finish(weights, stacks, acc, starts, top, skip, out, rows):
    cols = stacks[0].shape[2]
    n_in, count = len(stacks), len(starts)
    vmem = pl.BlockSpec(memory_space=pltpu.VMEM)
    hbm = pl.BlockSpec(memory_space=pltpu.HBM)
    extra = [] if out is None else [out]
    return pl.pallas_call(
        functools.partial(finish_body, n_in, starts, top, skip, len(extra)),
        in_specs=[vmem] * (n_in + 2) + [hbm] * len(extra),
        out_specs=hbm,
        out_shape=jax.ShapeDtypeStruct((E, rows, cols), jnp.float32),
        input_output_aliases={n_in + 2: 0} if extra else {},
        scratch_shapes=[
            pltpu.VMEM((count, E, SUB, cols), jnp.float32),
            pltpu.SemaphoreType.DMA((count,)),
        ],
        cost_estimate=pl.CostEstimate(
            flops=2 * weights.shape[0] * weights.shape[1] * count * cols,
            bytes_accessed=4 * count * SUB * cols * (n_in * stacks[0].shape[0] + 2 * E),
            transcendentals=0,
        ),
        compiler_params=pltpu.CompilerParams(vmem_limit_bytes=VMEM_LIMIT),
    )(weights, *stacks, acc, *extra)


class Plan:
    def __init__(self, n_pair, n_quad, rows):
        self.devices = n_pair * n_quad
        self.half = self.devices // 2
        groups = rows // SUB
        self.merged = list(range(groups - max(1, groups // 2), groups))
        self.plain = list(range(self.merged[0]))
        self.split = self.merged[0] * SUB
        far = list(range(n_pair // 2, n_pair))
        far = far[len(far) // 2 :] + far[: len(far) // 2]
        near = list(range(n_pair // 4, n_pair // 2))
        rest = list(range(n_pair // 4))[::-1]
        cut, middle = len(far) - len(far) // 4, len(near) // 2
        steps = [("far", mask) for mask in far[:cut]]
        steps += [("near", mask) for mask in near[:middle]]
        steps += [("far", mask) for mask in far[cut:]]
        steps += [("operator", None), ("merge", 0)]
        steps += [("near", mask) for mask in near[middle:]]
        steps += [("merge", k) for k in range(1, len(self.merged))]
        self.steps = steps + [("near", mask) for mask in rest]
        self.far = far


def shards(interferograms, pair_epochs, days):
    n_pair = lax.axis_size("pair")
    n_quad = lax.axis_size("quad")
    local, height, width = interferograms.shape
    rows = height // n_pair
    cols = width // n_quad
    plan = Plan(n_pair, n_quad, rows)
    half = plan.half
    state = [None, None]

    def smooth(mask, cuts):
        blocks, state[0], state[1] = smooth_rows(
            interferograms, mask, *state, rows, cols, cuts
        )
        return blocks

    def send(block, which):
        if which == 0:
            return block
        route = [(i, i ^ which) for i in range(plan.devices)]
        return lax.ppermute(block, AXES, route)

    plain, gathered, own, arrived = {}, {}, {}, []
    everyone = list(range(half))
    for kind, item in plan.steps:
        if kind == "far":
            blocks = smooth(item, (plan.split, rows - plan.split))
            for flip, (first, second) in enumerate(blocks):
                which = item * n_quad + flip
                plain[which] = send(first, which)
                gathered[which - half] = send(second, which - half)
        elif kind == "near":
            for flip, (block,) in enumerate(smooth(item, (rows,))):
                which = item * n_quad + flip
                own[which] = send(block, which)
        elif kind == "operator":
            whole, narrow, basis = temporal_operator(pair_epochs, days)
            weights = expand(narrow, everyone, local)
        else:
            stacks = [gathered[which] for which in everyone]
            some = apply_operator(weights, stacks, None, [item * SUB])
            arrived.append(send(some, half))
    total = None
    starts = [k * SUB for k in plan.plain]
    left = [mask * n_quad + flip for mask in plan.far for flip in range(n_quad)]
    weights = expand(whole, left, local)
    total = apply_operator(weights, [plain[w] for w in left], None, starts)
    weights = expand(whole, everyone, local)
    stacks = [own[w] for w in everyone]
    out = finish(weights, stacks, total, starts, 0, 0, None, rows)
    later = [k * SUB for k in plan.merged]
    total = apply_operator(weights, stacks, None, later)
    weights = expand(basis, None, local)
    for k, group in enumerate(plan.merged):
        top = group * SUB
        out = finish(weights, [arrived[k]], total, [0], top, k * SUB, out, rows)
    return out


def solution(mesh):
    placed = (P(("pair", "quad"), "slab", None), P(), P())

    def step(interferograms, pair_epochs, days):
        mapped = jax.shard_map(
            shards,
            mesh=mesh,
            in_specs=placed,
            out_specs=P(None, ("slab", "pair"), "quad"),
            check_vma=False,
        )
        return mapped(interferograms, pair_epochs, days)

    return step
```
